128 devices in a mesh: pipe: 4 (over z_hi, core), dp: 32 (over z_lo, x, y).
Axes of the slice: x: 4, y: 4, z: 4 (z_hi: 2, z_lo: 2; z = z_hi * 2 + z_lo), core: 2. Of those that a mesh axis runs over, the one named last changes fastest.
Arguments:
- frames_in: bfloat16 [64, 750, 1536], P('dp'), may hold values from -6 to 6
- lengths: int32 [64], P('dp'), may hold values from 375 to 750, as said below
- norm_gain: float32 [2, 4, 1536], P(None, 'pipe'), may hold values from 0.25 to 1.75
- lift_weight: bfloat16 [2, 4, 1536, 3072], P(None, 'pipe', 'dp'), may hold values from -0.15625 to 0.15625
- depth_kernel: float32 [2, 4, 31, 1536], P(None, 'pipe'), may hold values from -1 to 1
- out_gain: float32 [2, 4, 1536], P(None, 'pipe'), may hold values from 0.25 to 1.75
Outputs:
- frames_out: bfloat16 [64, 750, 1536], P('dp', None, 'pipe')
The draws below stay inside these ranges and needn't reach their ends.
Inputs may be any that keep to these rules, and one draw needn't show every extreme that they name: `lengths`: valid frames of each clip; in every draw at least one clip has all its frames valid.
All inputs are finite; a program needn't handle non-finite values.
Results may differ from the reference program's by a relative error of at most 0.022.
Values may be sent and summed in bfloat16 or wider, within the bound.
A program may use at most 128 MiB of HBM per device.

```python
import jax
import jax.numpy as jnp
from jax import lax

D = 1536
CONV_K = 31
FRAMES = 750
VIRT = 2
CLIPS = 64
N_PIPE = 4


def draw_lengths(key, part):
    first_key, second_key = jax.random.split(jax.random.fold_in(key, 11))
    drawn = jax.random.randint(first_key, (CLIPS,), FRAMES // 2, FRAMES + 1)
    chosen = jax.random.randint(second_key, (), 0, CLIPS)
    return jnp.where(jnp.arange(CLIPS) == chosen, FRAMES, drawn).astype(jnp.int32)


def block_levels(rng, dims, cuts, smallest, largest):
    def one(position, shards_of):
        steps = jax.random.uniform(jax.random.fold_in(jax.random.fold_in(rng, 6), position), (shards_of,), jnp.float32, smallest / len(cuts), largest / len(cuts))
        return jnp.repeat(jnp.exp(steps), dims[position] // shards_of).reshape((-1,) + (1,) * (len(dims) - position - 1))

    gain = one(*cuts[0])
    for cut in cuts[1:]:
        gain = gain * one(*cut)
    return gain


def noise(key, extent, scale, limit, cuts=(), kind=jnp.bfloat16):
    result = scale * jax.random.normal(key, extent, jnp.float32)
    if cuts:
        result = result * block_levels(key, extent, cuts, -0.22, 0.18)
    return jnp.clip(result, -limit, limit).astype(kind)


def setup_inputs(seed: int = 0) -> dict:
    arg_keys = jax.random.split(jax.random.key(seed), 7)
    return {
        "frames_in": noise(arg_keys[0], (CLIPS, FRAMES, D), 1.0, 6.0, ((0, 32),)),
        "lengths": draw_lengths(jax.random.fold_in(arg_keys[6], 71), 0),
        "norm_gain": jnp.clip(1.0 + 0.15 * jax.random.normal(arg_keys[2], (VIRT, N_PIPE, D), jnp.float32), 0.25, 1.75),
        "lift_weight": noise(arg_keys[3], (VIRT, N_PIPE, D, 2 * D), D ** -0.5, 0.15625, ((1, 4), (2, 32))),
        "depth_kernel": noise(arg_keys[4], (VIRT, N_PIPE, CONV_K, D), CONV_K ** -0.5, 1.0, ((1, 4),), jnp.float32),
        "out_gain": jnp.clip(1.0 + 0.15 * jax.random.normal(arg_keys[5], (VIRT, N_PIPE, D), jnp.float32), 0.25, 1.75),
    }


def layer_norm(values):
    centred = values - lax.optimization_barrier(jnp.mean(values, axis=-1, keepdims=True))
    return centred * lax.rsqrt(lax.optimization_barrier(jnp.mean(centred * centred, axis=-1, keepdims=True)) + 1e-05)

def conv_module(current, valid_mask, gain_in, lift_weight, kernel, gain_out):
    model_width = current.shape[-1]
    frame_count = current.shape[0]
    kernel_taps = kernel.shape[0]
    half_width = (kernel_taps - 1) // 2
    values = current.astype(jnp.float32)
    normed = (layer_norm(values) * gain_in).astype(jnp.bfloat16)
    lifted = jnp.dot(normed, lift_weight, preferred_element_type=jnp.float32)
    gated_rows = lifted[:, :model_width] * jax.nn.sigmoid(lifted[:, model_width:]) * valid_mask[:, None]
    padded = jnp.pad(gated_rows, ((half_width, half_width), (0, 0)))
    mixed_rows = padded[0:frame_count] * kernel[0]
    for offset in range(1, kernel_taps):
        mixed_rows = mixed_rows + padded[offset:offset + frame_count] * kernel[offset]
    branch = jax.nn.silu(layer_norm(mixed_rows) * gain_out)
    return (values + valid_mask[:, None] * branch).astype(jnp.bfloat16)

def reference(frames_in, lengths, norm_gain, lift_weight, depth_kernel, out_gain):
    positions = jnp.arange(FRAMES, dtype=jnp.int32)

    def one_clip(inputs):
        current, length_here = inputs
        valid_mask = (positions < length_here).astype(jnp.float32)
        for module_index in range(VIRT * N_PIPE):
            virt_index = module_index // N_PIPE
            section_index = module_index % N_PIPE
            current = conv_module(current, valid_mask, norm_gain[virt_index, section_index], lift_weight[virt_index, section_index], depth_kernel[virt_index, section_index], out_gain[virt_index, section_index])
        return current
    return lax.map(one_clip, (frames_in, lengths))
```

```python
import functools

import jax
import jax.numpy as jnp
from jax import lax
from jax.experimental import pallas as pl
from jax.experimental.pallas import tpu as pltpu
from jax.sharding import PartitionSpec as P

ROWS = 512; SEG = ROWS // 8; D = 1536; TAPS = 31; HALF = 15; EPS = 1e-5
f32 = jnp.float32

def sigm(v):
    return 1.0 / (1.0 + jnp.exp(-v))

class Module:
    def __init__(s, st, mask, prm, wb, norm, gpad, mix):
        s.st, s.mask, s.prm, s.wb, s.norm, s.gpad, s.mix = st, mask, prm, wb, norm, gpad, mix
    def ln1(s, m):
        gain = s.prm[lax.rem(m, 4), lax.div(m, 4), TAPS:TAPS + 1, :]
        @pl.loop(0, ROWS // 16)
        def _(r):
            rows = pl.ds(pl.multiple_of(r * 16, 16), 16)
            v = s.st[rows, :].astype(f32)
            v = v - jnp.mean(v, axis=-1, keepdims=True)
            q = lax.rsqrt(jnp.mean(v * v, axis=-1, keepdims=True) + EPS)
            s.norm[rows, :] = (v * q * gain).astype(jnp.bfloat16)
    def cols(s, m, j):
        slot = lax.rem(m, 2)
        ca = pl.ds(pl.multiple_of(j * 256, 256), 256); cb = pl.ds(pl.multiple_of(D + j * 256, 256), 256)
        wa = s.wb[slot, :, :, :, :, ca].reshape(D, 256)
        a = jnp.dot(s.norm[...], wa, preferred_element_type=f32)
        wg = s.wb[slot, :, :, :, :, cb].reshape(D, 256)
        b = jnp.dot(s.norm[...], wg, preferred_element_type=f32)
        sub = lax.broadcasted_iota(jnp.int32, (HALF, 8, 128), 1)
        for q in range(2):
            l = slice(q * 128, q * 128 + 128)
            g = (a[:, l] * sigm(b[:, l]) * s.mask[...]).reshape(SEG, 8, 128)
            s.gpad[q, 16:16 + SEG] = g
            s.gpad[q, 1:16] = jnp.where(sub == 0, 0.0, pltpu.roll(g[SEG - HALF:], 1, 1))
            s.gpad[q, 16 + SEG:16 + SEG + HALF] = jnp.where(sub == 7, 0.0, pltpu.roll(g[:HALF], 7, 1))
        NB = 8
        for q in range(2):
            lanes = pl.ds(pl.multiple_of(j * 256 + q * 128, 128), 128)
            @pl.loop(0, SEG // NB)
            def _(rb):
                base = rb * NB
                w = [jnp.broadcast_to(s.prm[lax.rem(m, 4), lax.div(m, 4), k:k + 1, lanes], (8, 128)) for k in range(TAPS)]
                acc = [None] * NB
                for t in range(NB + TAPS - 1):
                    x = s.gpad[q, base + 1 + t]
                    for o in range(NB):
                        k = t - o
                        if 0 <= k < TAPS:
                            acc[o] = x * w[k] if acc[o] is None else acc[o] + x * w[k]
                for o in range(NB):
                    s.mix[base + o, :, lanes] = acc[o]
    def ln2(s, m):
        gain = s.prm[lax.rem(m, 4), lax.div(m, 4), TAPS + 1:TAPS + 2, :]
        @pl.loop(0, ROWS // 16)
        def _(r):
            rows = pl.ds(pl.multiple_of(r * 16, 16), 16)
            v = s.mix[pl.ds(pl.multiple_of(r * 2, 2), 2)].reshape(16, D)
            v = v - jnp.mean(v, axis=-1, keepdims=True)
            q = lax.rsqrt(jnp.mean(v * v, axis=-1, keepdims=True) + EPS)
            y = v * q * gain
            s.st[rows, :] = (s.st[rows, :].astype(f32) + s.mask[rows, :1] * (y * sigm(y))).astype(jnp.bfloat16)
    def run(s, m):
        s.ln1(m)
        @pl.loop(0, 6)
        def _(j): s.cols(m, j)
        s.ln2(m)


SPLIT = (4, 5, 3)
MESH = pl.DeviceIdType.MESH

def div(a, b): return lax.div(a, jnp.int32(b))

def rem(a, b): return lax.rem(a, jnp.int32(b))

def coords():
    pipe = lax.axis_index("pipe"); dp = lax.axis_index("dp")
    return rem(div(dp, 4), 4), rem(dp, 4), div(pipe, 2) * 2 + div(dp, 16), rem(pipe, 2)

def dev(x, y, z, core):
    return {"pipe": div(z, 2) * 2 + core, "dp": rem(z, 2) * 16 + x * 4 + y}

class Ring:
    def __init__(s, pos, at, unit, half, present, send, recv):
        s.pos, s.at, s.unit, s.half, s.present, s.send, s.recv = pos, at, unit, half, present, send, recv
    def copy(s, k, src, to):
        return pltpu.make_async_remote_copy(src, src, s.send.at[k], s.recv.at[k], device_id=s.at(to), device_id_type=MESH)
    def sends(s):
        p = s.pos; up, dn = rem(p + 1, 4), rem(p + 3, 4)
        return [(s.present(p), lambda: s.copy(0, s.unit(p), up)), (s.present(p), lambda: s.copy(1, s.unit(p), dn)),
                (s.present(dn), lambda: s.copy(2, s.half(dn, 0), up)), (s.present(up), lambda: s.copy(3, s.half(up, 1), dn))]
    def recvs(s):
        p = s.pos; up, dn, op = rem(p + 1, 4), rem(p + 3, 4), rem(p + 2, 4)
        return [(s.present(dn), lambda: s.copy(0, s.unit(dn), up)), (s.present(up), lambda: s.copy(1, s.unit(up), dn)),
                (s.present(op), lambda: s.copy(2, s.half(op, 0), up)), (s.present(op), lambda: s.copy(3, s.half(op, 1), dn))]

def do(item, what):
    cond, mk = item
    if cond is True:
        getattr(mk(), what)()
    else:
        @pl.when(cond)
        def _(): getattr(mk(), what)()

class Gather:
    def __init__(s, w_ref, full, sems):
        s.w, s.full = w_ref, full
        s.x, s.y, s.z, s.core = coords()
        s.zl, s.zh = rem(s.z, 2), div(s.z, 2)
        s.sec = s.zh * 2 + s.core
        (s.own_sem, s.zs, s.zr, s.cs, s.cr, s.ms, s.mr, s.fs, s.fr, s.ds, s.dr) = sems
    def cols(s, part, n=1, core=None):
        core = s.core if core is None else core
        return pl.ds(pl.multiple_of(core * 1536 + 128 * sum(SPLIT[:part]), 128), 128 * sum(SPLIT[part:part + n]))
    def peers(s):
        x, y, z, c = s.x, s.y, s.z, s.core
        r = [dev(x, y, z, 1 - c)]
        r += [dev(rem(x + d, 4), y, z, c) for d in (1, 2, 3)]
        r += [dev(x, rem(y + d, 4), z, c) for d in (1, 3)]
        r += [dev(x, y, rem(z + d, 4), c) for d in (1, 2, 3)]
        r += [dev(x, y, rem(z + 2, 4), 1 - c)]
        return r
    def own_copies(s):
        o = 1 - s.core
        mine, other = s.cols(0, 3), s.cols(0, 3, o)
        here = s.full.at[:, s.sec, s.zl, s.x, s.y]
        return (pltpu.make_async_copy(s.w.at[:, :, mine], here.at[:, :, mine], s.own_sem.at[0]),
                pltpu.make_async_remote_copy(s.w.at[:, :, other], here.at[:, :, other], s.own_sem.at[1], s.own_sem.at[2], device_id=dev(s.x, s.y, s.z, o), device_id_type=MESH))
    def own_arrival(s):
        mine = s.cols(0, 3)
        there = s.full.at[:, s.zh * 2 + 1 - s.core, s.zl, s.x, s.y]
        return pltpu.make_async_remote_copy(s.w.at[:, :, mine], there.at[:, :, mine], s.own_sem.at[1], s.own_sem.at[2], device_id=dev(s.x, s.y, s.z, 1 - s.core), device_id_type=MESH)
    def begin(s):
        a, b = s.own_copies()
        a.start(); b.start(); a.wait(); b.wait_send(); s.own_arrival().wait_recv()
    def mod(s, c):
        return s.full.at[div(c, 4), rem(c, 4)]
    def src(s, c):
        return s.zh == div(rem(c, 4), 2)
    def first_sends(s, c):
        W = s.mod(c); out = []
        for d in (1, 2, 3):
            out.append((s.src(c), functools.partial(s.zcopy, W, c, s.zl, d - 1, rem(s.z + d, 4))))
        for d in (1, 2, 3):
            out.append((s.src(c), functools.partial(s.ccopy, W, c, s.x, d - 1, rem(s.x + d, 4))))
        return out
    def zcopy(s, W, c, zl, k, to):
        sl = W.at[zl, s.x, s.y, :, s.cols(0, 2)]
        return pltpu.make_async_remote_copy(sl, sl, s.zs.at[c, k], s.zr.at[c, zl], device_id=dev(s.x, s.y, to, s.core), device_id_type=MESH)
    def ccopy(s, W, c, q, k, to):
        sl = W.at[s.zl, q, s.y, :, s.cols(2)]
        return pltpu.make_async_remote_copy(sl, sl, s.cs.at[c, k], s.cr.at[c, k], device_id=dev(to, s.y, s.z, s.core), device_id_type=MESH)
    def first_recvs(s, c):
        W = s.mod(c); out = []
        for zl in (0, 1):
            out.append((jnp.logical_not(jnp.logical_and(s.src(c), s.zl == zl)), functools.partial(s.zcopy, W, c, zl, 0, s.z)))
        for d in (1, 2, 3):
            out.append((s.src(c), functools.partial(s.ccopy, W, c, rem(s.x + 4 - d, 4), d - 1, s.x)))
        return out
    def mids(s, c):
        W = s.mod(c); yes = lambda q: True; src = lambda q: s.src(c)
        a, b, cc = s.cols(0), s.cols(1), s.cols(2)
        atx = lambda q: dev(q, s.y, s.z, s.core)
        aty = lambda q: dev(s.x, q, s.z, s.core)
        return [Ring(s.x, atx, lambda q: W.at[:, q, s.y, :, a], lambda q, h: W.at[h, q, s.y, :, a], yes, s.ms.at[c, 0], s.mr.at[c, 0]),
                Ring(s.y, aty, lambda q: W.at[:, s.x, q, :, b], lambda q, h: W.at[h, s.x, q, :, b], yes, s.ms.at[c, 1], s.mr.at[c, 1]),
                Ring(s.y, aty, lambda q: W.at[s.zl, :, q, :, cc], lambda q, h: W.at[s.zl, pl.ds(2 * h, 2), q, :, cc], src, s.ms.at[c, 2], s.mr.at[c, 2])]
    def fins(s, c):
        W = s.mod(c); yes = lambda q: True
        a, b, cc = s.cols(0), s.cols(1), s.cols(2)
        atx = lambda q: dev(q, s.y, s.z, s.core)
        aty = lambda q: dev(s.x, q, s.z, s.core)
        atz = lambda q: dev(s.x, s.y, q, s.core)
        return [Ring(s.y, aty, lambda q: W.at[:, :, q, :, a], lambda q, h: W.at[h, :, q, :, a], yes, s.fs.at[c, 0], s.fr.at[c, 0]),
                Ring(s.x, atx, lambda q: W.at[:, q, :, :, b], lambda q, h: W.at[h, q, :, :, b], yes, s.fs.at[c, 1], s.fr.at[c, 1]),
                Ring(s.z, atz, lambda q: W.at[rem(q, 2), :, :, :, cc], lambda q, h: W.at[rem(q, 2), pl.ds(2 * h, 2), :, :, cc],
                     lambda q: div(q, 2) == div(rem(c, 4), 2), s.fs.at[c, 2], s.fr.at[c, 2])]
    def swap(s, c, part, core):
        sl = s.mod(c).at[:, :, :, :, s.cols(part, 1, core)]
        return pltpu.make_async_remote_copy(sl, sl, s.ds.at[c, part], s.dr.at[c, part], device_id=dev(s.x, s.y, s.z, 1 - s.core), device_id_type=MESH)
    def e1(s, c):
        for it in s.first_sends(c): do(it, "start")
    def e2(s, c):
        for it in s.first_recvs(c): do(it, "wait_recv")
        for r in s.mids(c):
            for it in r.sends()[:2]: do(it, "start")
    def relay(s, rings):
        for k in (0, 1):
            for r in rings:
                do(r.recvs()[k], "wait_recv"); do(r.sends()[2 + k], "start")
    def e3(s, c): s.relay(s.mids(c))
    def e4(s, c):
        for r, f in zip(s.mids(c), s.fins(c)):
            for it in r.recvs()[2:]: do(it, "wait_recv")
            for it in f.sends()[:2]: do(it, "start")
    def e5a(s, c): s.relay(s.fins(c))
    def e5b(s, c):
        for p, r in enumerate(s.fins(c)):
            for it in r.recvs()[2:]: do(it, "wait_recv")
            s.swap(c, p, s.core).start()
    def e6(s, c):
        for p in range(3): s.swap(c, p, 1 - s.core).wait_recv()
    def drain(s, c):
        for it in s.first_sends(c): do(it, "wait_send")
        for r in s.mids(c) + s.fins(c):
            for it in r.sends(): do(it, "wait_send")
        for p in range(3): s.swap(c, p, s.core).wait_send()


NG = 5

def guard(m, fn):
    @pl.when(jnp.logical_and(m >= 0, m < 8))
    def _(): fn(m)

class Shares:
    def __init__(s, g, send, recv, own):
        s.g, s.send, s.recv, s.own = g, send, recv, own
    def at(s, pipe):
        return {"pipe": pipe}
    def each(s, src_of, dst_of, what):
        me = s.g.sec
        for q in range(4):
            if what == "start":
                @pl.when(me != q)
                def _(): pltpu.make_async_remote_copy(src_of(q), dst_of(me), s.send.at[q], s.recv.at[me], device_id={"pipe": q}, device_id_type=MESH).start()
                @pl.when(me == q)
                def _(): pltpu.make_async_copy(src_of(q), dst_of(me), s.own).start()
            else:
                @pl.when(me != q)
                def _():
                    pltpu.make_async_remote_copy(src_of(q), dst_of(me), s.send.at[q], s.recv.at[me], device_id={"pipe": q}, device_id_type=MESH).wait_send()
                    pltpu.make_async_remote_copy(src_of(q), dst_of(q), s.send.at[q], s.recv.at[q], device_id={"pipe": q}, device_id_type=MESH).wait_recv()
                @pl.when(me == q)
                def _(): pltpu.make_async_copy(src_of(q), dst_of(me), s.own).wait()

def kernel(x_ref, mask_ref, prm_ref, w_ref, out_ref, full, st, wb, norm, gpad, mix, wsem, prm, ps, pr, po, os_, or_, oo, *sems):
    g = Gather(w_ref, full, sems)
    b = pltpu.get_barrier_semaphore()
    for d in g.peers():
        pl.semaphore_signal(b, inc=1, device_id=d, device_id_type=MESH)
    pl.semaphore_wait(b, len(g.peers()))
    shares = Shares(g, ps, pr, po)
    psrc, pdst = (lambda q: prm_ref), (lambda q: prm.at[q])
    g.begin()
    g.e1(jnp.int32(0))
    shares.each(psrc, pdst, "start")
    st[...] = x_ref[...]
    md = Module(st, mask_ref, prm, wb, norm, gpad, mix)
    load = lambda m: pltpu.make_async_copy(full.at[div(m, 4), rem(m, 4)], wb.at[rem(m, 2)], wsem.at[rem(m, 2)])
    def head(m):
        g.e6(m); load(m).start()
        @pl.when(m == 0)
        def _(): shares.each(psrc, pdst, "wait")
        md.ln1(m)
    def some(m, lo, hi):
        @pl.loop(lo, hi)
        def _(j): md.cols(m, j)
    @pl.loop(0, 14)
    def _(i):
        m = i - 6
        guard(m, head)
        @pl.when(i > 0)
        def _(): guard(i, g.e1)
        guard(i - 1, g.e2)
        guard(m, lambda m: load(m).wait())
        guard(m, lambda m: some(m, 0, 2))
        guard(i - 2, g.e3)
        guard(m, lambda m: some(m, 2, 3))
        guard(i - 3, g.e4)
        guard(m, lambda m: some(m, 3, 5))
        guard(i - 4, g.e5a)
        guard(m, lambda m: some(m, 5, 6))
        guard(m, md.ln2)
        guard(i - 5, g.e5b)
    outs = Shares(g, os_, or_, oo)
    osrc, odst = (lambda q: st.at[:, pl.ds(q * (D // 4), D // 4)]), (lambda q: out_ref.at[q])
    outs.each(osrc, odst, "start")
    @pl.loop(0, 8)
    def _(i): g.drain(i)
    outs.each(osrc, odst, "wait")

SEM = pltpu.SemaphoreType.DMA
V = pltpu.VMEM

def run(x, mask, prm, w):
    vm, hbm = pl.BlockSpec(memory_space=pltpu.VMEM), pl.BlockSpec(memory_space=pl.ANY)
    return pl.pallas_call(
        kernel,
        out_shape=(jax.ShapeDtypeStruct((4, ROWS, D // 4), jnp.bfloat16), jax.ShapeDtypeStruct((2, 4, 2, 4, 4, 48, 2 * D), jnp.bfloat16)),
        in_specs=[vm, vm, vm, vm],
        out_specs=(hbm, hbm),
        scratch_shapes=[
            V((ROWS, D), jnp.bfloat16), V((2, 2, 4, 4, 48, 2 * D), jnp.bfloat16), V((ROWS, D), jnp.bfloat16),
            V((2, 16 + SEG + 16, 8, 128), f32), V((SEG, 8, D), f32), SEM((2,)), V((4, 2, 40, D), f32),
            SEM((4,)), SEM((4,)), SEM, SEM((4,)), SEM((4,)), SEM,
            SEM((3,)), SEM((8, 3)), SEM((8, 2)), SEM((8, 3)), SEM((8, 3)), SEM((8, 3, 4)), SEM((8, 3, 4)), SEM((8, 3, 4)), SEM((8, 3, 4)), SEM((8, 3)), SEM((8, 3)),
        ],
        compiler_params=pltpu.CompilerParams(collective_id=0, has_side_effects=True, vmem_limit_bytes=60 * 2**20),
    )(x, mask, prm, w)[0]

def on_device(frames_in, lengths, norm_gain, lift_weight, depth_kernel, out_gain):
    frames = frames_in.shape[1]
    pipe = lax.axis_index("pipe")
    clip, half = pipe // 2, pipe % 2
    late = frames - ROWS
    p = jnp.arange(ROWS, dtype=jnp.int32)
    local = p % 8 * SEG + p // 8
    when = local + half * late
    pick = (when[:, None] == jnp.arange(frames, dtype=jnp.int32)[None]).astype(jnp.bfloat16)
    mine = lax.dynamic_index_in_dim(frames_in, clip, 0, keepdims=False)
    x = jnp.dot(pick, mine, preferred_element_type=f32).astype(jnp.bfloat16)
    length = lax.dynamic_index_in_dim(lengths, clip, 0, keepdims=False)
    mask = jnp.broadcast_to((when < length).astype(f32)[:, None], (ROWS, 128))
    prm = jnp.concatenate([depth_kernel[:, 0], norm_gain, out_gain, jnp.zeros((2, 7, D), f32)], axis=1)
    got = run(x, mask, prm, lift_weight[:, 0])
    t = jnp.arange(frames, dtype=jnp.int32)
    cut = frames // 2
    source = jnp.where(t < cut, local_row(t), ROWS + local_row(t - late))
    back = (source[:, None] == jnp.arange(2 * ROWS, dtype=jnp.int32)[None]).astype(jnp.bfloat16)
    got = got.reshape(2, 2 * ROWS, D // 4)
    return jnp.stack([jnp.dot(back, got[c], preferred_element_type=f32).astype(jnp.bfloat16) for c in range(2)])

def local_row(t):
    return t % SEG * 8 + t // SEG

def solution(mesh):
    return jax.shard_map(
        on_device,
        mesh=mesh,
        in_specs=(P("dp", None, None), P("dp"), P(None, "pipe", None), P(None, "pipe", "dp", None), P(None, "pipe", None, None), P(None, "pipe", None)),
        out_specs=P("dp", None, "pipe"),
        check_vma=False,
    )
```

```python
import functools

import jax
import jax.numpy as jnp
from jax import lax
from jax.experimental import pallas as pl
from jax.experimental.pallas import tpu as pltpu
from jax.sharding import PartitionSpec as P

ROWS = 512; LANES = 16; SEG = ROWS // LANES; D = 1536; TAPS = 31; HALF = 15; EPS = 1e-5
f32 = jnp.float32
bf16 = jnp.bfloat16
GROUP, NB = 8, 8

def sigm(v):
    return 1.0 / (1.0 + jnp.exp(-v))

class Module:
    def __init__(s, st, mask, prm, wb, norm, gpads, mix):
        s.st, s.mask, s.prm, s.wb, s.norm, s.gpads, s.mix = st, mask, prm, wb, norm, gpads, mix
    def par(s, m, row, n=1):
        return s.prm.at[lax.rem(m, jnp.int32(4)), lax.div(m, jnp.int32(4)), row:row + n]
    def ln1(s, m):
        gain = s.par(m, TAPS)[...]
        @pl.loop(0, ROWS // 32)
        def _(r):
            for h in range(2):
                rows = pl.ds(pl.multiple_of(r * 32 + h * 16, 16), 16)
                v = s.st[rows, :].astype(f32)
                v = v - jnp.mean(v, axis=-1, keepdims=True)
                q = lax.rsqrt(jnp.mean(v * v, axis=-1, keepdims=True) + EPS) * s.mask[rows, :1]
                s.norm[rows, :] = (v * q * gain).astype(bf16)
    def lift(s, m, j):
        slot = lax.rem(m, jnp.int32(2)); pad = s.gpads[j % 2]
        w = lambda c: s.wb[slot, :, :, :, :, c:c + 256].reshape(D, 256)
        a = jnp.dot(s.norm[...], w(j * 256), preferred_element_type=f32)
        b = jnp.dot(s.norm[...], w(D + j * 256), preferred_element_type=f32)
        sub = lax.broadcasted_iota(jnp.int32, (HALF, LANES, 128), 1)
        for q in range(2):
            l = slice(q * 128, q * 128 + 128)
            g = (a[:, l] * sigm(b[:, l])).reshape(SEG, LANES, 128)
            pad[q, 16:16 + SEG] = g
            pad[q, 1:16] = jnp.where(sub == 0, 0.0, pltpu.roll(g[SEG - HALF:], 1, 1))
            pad[q, 16 + SEG:31 + SEG] = jnp.where(sub == LANES - 1, 0.0, pltpu.roll(g[:HALF], LANES - 1, 1))
    def conv(s, m, j):
        pad = s.gpads[j % 2]
        for q in range(2):
            c = slice(j * 256 + q * 128, j * 256 + q * 128 + 128)
            taps = s.par(m, 0, 32)
            w = [jnp.broadcast_to(taps[k:k + 1, c], (LANES, 128)).astype(bf16) for k in range(TAPS)]
            for base in range(0, SEG, NB):
                acc = [None] * NB
                x = {}
                for k0 in range(0, TAPS, GROUP):
                    ks = range(k0, min(TAPS, k0 + GROUP))
                    for t in range(k0, k0 + len(ks) + NB - 1):
                        if t not in x: x[t] = pad[q, base + 1 + t].astype(bf16)
                    for o in range(NB):
                        p = None
                        for k in ks:
                            p = x[o + k] * w[k] if p is None else p + x[o + k] * w[k]
                        p = p.astype(f32)
                        acc[o] = p if acc[o] is None else acc[o] + p
                for o in range(NB):
                    s.mix[base + o, :, c] = acc[o]
    def ln2(s, m):
        gain = s.par(m, TAPS + 1)[...]
        @pl.loop(0, ROWS // 32)
        def _(r):
            for h in range(2):
                rows = pl.ds(pl.multiple_of(r * 32 + h * 16, 16), 16)
                v = s.mix[r * 2 + h]
                v = v - jnp.mean(v, axis=-1, keepdims=True)
                q = lax.rsqrt(jnp.mean(v * v, axis=-1, keepdims=True) + EPS)
                y = v * q * gain
                s.st[rows, :] = (s.st[rows, :].astype(f32) + s.mask[rows, :1] * (y * sigm(y))).astype(bf16)
    def stage(s, m, j):
        if j > 0: s.conv(m, j - 1)
        if j < 6: s.lift(m, j)
    def run(s, m):
        s.ln1(m)
        for j in range(7): s.stage(m, j)
        s.ln2(m)


SPLIT = (4, 5, 3)
MESH = pl.DeviceIdType.MESH

def div(a, b): return lax.div(a, jnp.int32(b))

def rem(a, b): return lax.rem(a, jnp.int32(b))

def coords():
    pipe = lax.axis_index("pipe"); dp = lax.axis_index("dp")
    return rem(div(dp, 4), 4), rem(dp, 4), div(pipe, 2) * 2 + div(dp, 16), rem(pipe, 2)

def dev(x, y, z, core):
    return {"pipe": div(z, 2) * 2 + core, "dp": rem(z, 2) * 16 + x * 4 + y}

class Ring:
    def __init__(s, pos, at, unit, half, present, send, recv):
        s.pos, s.at, s.unit, s.half, s.present, s.send, s.recv = pos, at, unit, half, present, send, recv
    def copy(s, k, src, to):
        return pltpu.make_async_remote_copy(src, src, s.send.at[k], s.recv.at[k], device_id=s.at(to), device_id_type=MESH)
    def sends(s):
        p = s.pos; up, dn = rem(p + 1, 4), rem(p + 3, 4)
        return [(s.present(p), lambda: s.copy(0, s.unit(p), up)), (s.present(p), lambda: s.copy(1, s.unit(p), dn)),
                (s.present(dn), lambda: s.copy(2, s.half(dn, 0), up)), (s.present(up), lambda: s.copy(3, s.half(up, 1), dn))]
    def recvs(s):
        p = s.pos; up, dn, op = rem(p + 1, 4), rem(p + 3, 4), rem(p + 2, 4)
        return [(s.present(dn), lambda: s.copy(0, s.unit(dn), up)), (s.present(up), lambda: s.copy(1, s.unit(up), dn)),
                (s.present(op), lambda: s.copy(2, s.half(op, 0), up)), (s.present(op), lambda: s.copy(3, s.half(op, 1), dn))]

def do(item, what):
    cond, mk = item
    if cond is True:
        getattr(mk(), what)()
    else:
        @pl.when(cond)
        def _(): getattr(mk(), what)()

class Gather:
    def __init__(s, w_ref, full, sems):
        s.w, s.full = w_ref, full
        s.x, s.y, s.z, s.core = coords()
        s.zl, s.zh = rem(s.z, 2), div(s.z, 2)
        s.sec = s.zh * 2 + s.core
        (s.own_sem, s.zs, s.zr, s.cs, s.cr, s.ms, s.mr, s.fs, s.fr, s.ds, s.dr) = sems
    def cols(s, part, n=1, core=None):
        core = s.core if core is None else core
        return pl.ds(pl.multiple_of(core * 1536 + 128 * sum(SPLIT[:part]), 128), 128 * sum(SPLIT[part:part + n]))
    def peers(s):
        x, y, z, c = s.x, s.y, s.z, s.core
        r = [dev(x, y, z, 1 - c)]
        r += [dev(rem(x + d, 4), y, z, c) for d in (1, 2, 3)]
        r += [dev(x, rem(y + d, 4), z, c) for d in (1, 3)]
        r += [dev(x, y, rem(z + d, 4), c) for d in (1, 2, 3)]
        r += [dev(x, y, rem(z + 2, 4), 1 - c)]
        return r
    def own_copies(s):
        o = 1 - s.core
        mine, other = s.cols(0, 3), s.cols(0, 3, o)
        here = s.full.at[:, s.sec, s.zl, s.x, s.y]
        return (pltpu.make_async_copy(s.w.at[:, :, mine], here.at[:, :, mine], s.own_sem.at[0]),
                pltpu.make_async_remote_copy(s.w.at[:, :, other], here.at[:, :, other], s.own_sem.at[1], s.own_sem.at[2], device_id=dev(s.x, s.y, s.z, o), device_id_type=MESH))
    def own_arrival(s):
        mine = s.cols(0, 3)
        there = s.full.at[:, s.zh * 2 + 1 - s.core, s.zl, s.x, s.y]
        return pltpu.make_async_remote_copy(s.w.at[:, :, mine], there.at[:, :, mine], s.own_sem.at[1], s.own_sem.at[2], device_id=dev(s.x, s.y, s.z, 1 - s.core), device_id_type=MESH)
    def begin(s):
        a, b = s.own_copies()
        a.start(); b.start(); a.wait(); b.wait_send(); s.own_arrival().wait_recv()
    def mod(s, c):
        return s.full.at[div(c, 4), rem(c, 4)]
    def src(s, c):
        return s.zh == div(rem(c, 4), 2)
    def first_sends(s, c):
        W = s.mod(c); out = []
        for d in (1, 2, 3):
            out.append((s.src(c), functools.partial(s.zcopy, W, c, s.zl, d - 1, rem(s.z + d, 4))))
        for d in (1, 2, 3):
            out.append((s.src(c), functools.partial(s.ccopy, W, c, s.x, d - 1, rem(s.x + d, 4))))
        return out
    def zcopy(s, W, c, zl, k, to):
        sl = W.at[zl, s.x, s.y, :, s.cols(0, 2)]
        return pltpu.make_async_remote_copy(sl, sl, s.zs.at[c, k], s.zr.at[c, zl], device_id=dev(s.x, s.y, to, s.core), device_id_type=MESH)
    def ccopy(s, W, c, q, k, to):
        sl = W.at[s.zl, q, s.y, :, s.cols(2)]
        return pltpu.make_async_remote_copy(sl, sl, s.cs.at[c, k], s.cr.at[c, k], device_id=dev(to, s.y, s.z, s.core), device_id_type=MESH)
    def first_recvs(s, c):
        W = s.mod(c); out = []
        for zl in (0, 1):
            out.append((jnp.logical_not(jnp.logical_and(s.src(c), s.zl == zl)), functools.partial(s.zcopy, W, c, zl, 0, s.z)))
        for d in (1, 2, 3):
            out.append((s.src(c), functools.partial(s.ccopy, W, c, rem(s.x + 4 - d, 4), d - 1, s.x)))
        return out
    def mids(s, c):
        W = s.mod(c); yes = lambda q: True; src = lambda q: s.src(c)
        a, b, cc = s.cols(0), s.cols(1), s.cols(2)
        atx = lambda q: dev(q, s.y, s.z, s.core)
        aty = lambda q: dev(s.x, q, s.z, s.core)
        return [Ring(s.x, atx, lambda q: W.at[:, q, s.y, :, a], lambda q, h: W.at[h, q, s.y, :, a], yes, s.ms.at[c, 0], s.mr.at[c, 0]),
                Ring(s.y, aty, lambda q: W.at[:, s.x, q, :, b], lambda q, h: W.at[h, s.x, q, :, b], yes, s.ms.at[c, 1], s.mr.at[c, 1]),
                Ring(s.y, aty, lambda q: W.at[s.zl, :, q, :, cc], lambda q, h: W.at[s.zl, pl.ds(2 * h, 2), q, :, cc], src, s.ms.at[c, 2], s.mr.at[c, 2])]
    def fins(s, c):
        W = s.mod(c); yes = lambda q: True
        a, b, cc = s.cols(0), s.cols(1), s.cols(2)
        atx = lambda q: dev(q, s.y, s.z, s.core)
        aty = lambda q: dev(s.x, q, s.z, s.core)
        atz = lambda q: dev(s.x, s.y, q, s.core)
        return [Ring(s.y, aty, lambda q: W.at[:, :, q, :, a], lambda q, h: W.at[h, :, q, :, a], yes, s.fs.at[c, 0], s.fr.at[c, 0]),
                Ring(s.x, atx, lambda q: W.at[:, q, :, :, b], lambda q, h: W.at[h, q, :, :, b], yes, s.fs.at[c, 1], s.fr.at[c, 1]),
                Ring(s.z, atz, lambda q: W.at[rem(q, 2), :, :, :, cc], lambda q, h: W.at[rem(q, 2), pl.ds(2 * h, 2), :, :, cc],
                     lambda q: div(q, 2) == div(rem(c, 4), 2), s.fs.at[c, 2], s.fr.at[c, 2])]
    def swap(s, c, part, core):
        sl = s.mod(c).at[:, :, :, :, s.cols(part, 1, core)]
        return pltpu.make_async_remote_copy(sl, sl, s.ds.at[c, part], s.dr.at[c, part], device_id=dev(s.x, s.y, s.z, 1 - s.core), device_id_type=MESH)
    def e1(s, c):
        for it in s.first_sends(c): do(it, "start")
    def e2(s, c):
        for it in s.first_recvs(c): do(it, "wait_recv")
        for r in s.mids(c):
            for it in r.sends()[:2]: do(it, "start")
    def relay(s, rings):
        for k in (0, 1):
            for r in rings:
                do(r.recvs()[k], "wait_recv"); do(r.sends()[2 + k], "start")
    def e3(s, c): s.relay(s.mids(c))
    def e4(s, c):
        for r, f in zip(s.mids(c), s.fins(c)):
            for it in r.recvs()[2:]: do(it, "wait_recv")
            for it in f.sends()[:2]: do(it, "start")
    def e5a(s, c): s.relay(s.fins(c))
    def e5b(s, c):
        for p, r in enumerate(s.fins(c)):
            for it in r.recvs()[2:]: do(it, "wait_recv")
            s.swap(c, p, s.core).start()
    def e6(s, c):
        for p in range(3): s.swap(c, p, 1 - s.core).wait_recv()
    def drain(s, c):
        for it in s.first_sends(c): do(it, "wait_send")
        for r in s.mids(c) + s.fins(c):
            for it in r.sends(): do(it, "wait_send")
        for p in range(3): s.swap(c, p, s.core).wait_send()


def guard(m, fn):
    @pl.when(jnp.logical_and(m >= 0, m < 8))
    def _(): fn(m)

class Shares:
    def __init__(s, g, send, recv, own):
        s.g, s.send, s.recv, s.own = g, send, recv, own
    def at(s, pipe):
        return {"pipe": pipe}
    def each(s, src_of, dst_of, what):
        me = s.g.sec
        for q in range(4):
            if what == "start":
                @pl.when(me != q)
                def _(): pltpu.make_async_remote_copy(src_of(q), dst_of(me), s.send.at[q], s.recv.at[me], device_id={"pipe": q}, device_id_type=MESH).start()
                @pl.when(me == q)
                def _(): pltpu.make_async_copy(src_of(q), dst_of(me), s.own).start()
            else:
                @pl.when(me != q)
                def _():
                    pltpu.make_async_remote_copy(src_of(q), dst_of(me), s.send.at[q], s.recv.at[me], device_id={"pipe": q}, device_id_type=MESH).wait_send()
                    pltpu.make_async_remote_copy(src_of(q), dst_of(q), s.send.at[q], s.recv.at[q], device_id={"pipe": q}, device_id_type=MESH).wait_recv()
                @pl.when(me == q)
                def _(): pltpu.make_async_copy(src_of(q), dst_of(me), s.own).wait()

def kernel(x_ref, mask_ref, prm_ref, w_ref, out_ref, full, st, wb, norm, gpa, gpb, mix, wsem, prm, ps, pr, po, os_, or_, oo, *sems):
    g = Gather(w_ref, full, sems)
    b = pltpu.get_barrier_semaphore()
    for d in g.peers():
        pl.semaphore_signal(b, inc=1, device_id=d, device_id_type=MESH)
    pl.semaphore_wait(b, len(g.peers()))
    shares = Shares(g, ps, pr, po)
    psrc, pdst = (lambda q: prm_ref), (lambda q: prm.at[q])
    g.begin()
    g.e1(jnp.int32(0))
    shares.each(psrc, pdst, "start")
    st[...] = x_ref[...]
    md = Module(st, mask_ref, prm, wb, norm, (gpa, gpb), mix)
    load = lambda m: pltpu.make_async_copy(full.at[div(m, 4), rem(m, 4)], wb.at[rem(m, 2)], wsem.at[rem(m, 2)])
    def head(m):
        g.e6(m); load(m).start()
        @pl.when(m == 0)
        def _(): shares.each(psrc, pdst, "wait")
        md.ln1(m)
    def some(m, lo, hi):
        for j in range(lo, hi): md.stage(m, j)
    @pl.loop(0, 14)
    def _(i):
        m = i - 6
        guard(m, head)
        @pl.when(i > 0)
        def _(): guard(i, g.e1)
        guard(i - 1, g.e2)
        guard(m, lambda m: load(m).wait())
        guard(m, lambda m: some(m, 0, 2))
        guard(i - 2, g.e3)
        guard(m, lambda m: some(m, 2, 4))
        guard(i - 3, g.e4)
        guard(m, lambda m: some(m, 4, 5))
        guard(i - 4, g.e5a)
        guard(m, lambda m: some(m, 5, 7))
        guard(m, md.ln2)
        guard(i - 5, g.e5b)
    outs = Shares(g, os_, or_, oo)
    osrc, odst = (lambda q: st.at[:, pl.ds(q * (D // 4), D // 4)]), (lambda q: out_ref.at[q])
    outs.each(osrc, odst, "start")
    @pl.loop(0, 8)
    def _(i): g.drain(i)
    outs.each(osrc, odst, "wait")

SEM = pltpu.SemaphoreType.DMA
V = pltpu.VMEM

def run(x, mask, prm, w):
    vm, hbm = pl.BlockSpec(memory_space=pltpu.VMEM), pl.BlockSpec(memory_space=pl.ANY)
    return pl.pallas_call(
        kernel,
        out_shape=(jax.ShapeDtypeStruct((4, ROWS, D // 4), jnp.bfloat16), jax.ShapeDtypeStruct((2, 4, 2, 4, 4, 48, 2 * D), jnp.bfloat16)),
        in_specs=[vm, vm, vm, vm],
        out_specs=(hbm, hbm),
        scratch_shapes=[
            V((ROWS, D), jnp.bfloat16), V((2, 2, 4, 4, 48, 2 * D), jnp.bfloat16), V((ROWS, D), jnp.bfloat16),
            V((2, 32 + SEG, LANES, 128), f32), V((2, 32 + SEG, LANES, 128), f32), V((SEG, LANES, D), f32), SEM((2,)), V((4, 2, 40, D), f32),
            SEM((4,)), SEM((4,)), SEM, SEM((4,)), SEM((4,)), SEM,
            SEM((3,)), SEM((8, 3)), SEM((8, 2)), SEM((8, 3)), SEM((8, 3)), SEM((8, 3, 4)), SEM((8, 3, 4)), SEM((8, 3, 4)), SEM((8, 3, 4)), SEM((8, 3)), SEM((8, 3)),
        ],
        compiler_params=pltpu.CompilerParams(collective_id=0, has_side_effects=True, vmem_limit_bytes=60 * 2**20),
    )(x, mask, prm, w)[0]

def on_device(frames_in, lengths, norm_gain, lift_weight, depth_kernel, out_gain):
    frames = frames_in.shape[1]
    pipe = lax.axis_index("pipe")
    clip, half = pipe // 2, pipe % 2
    late = frames - ROWS
    p = jnp.arange(ROWS, dtype=jnp.int32)
    local = p % LANES * SEG + p // LANES
    when = local + half * late
    pick = (when[:, None] == jnp.arange(frames, dtype=jnp.int32)[None]).astype(jnp.bfloat16)
    mine = lax.dynamic_index_in_dim(frames_in, clip, 0, keepdims=False)
    x = jnp.dot(pick, mine, preferred_element_type=f32).astype(jnp.bfloat16)
    length = lax.dynamic_index_in_dim(lengths, clip, 0, keepdims=False)
    mask = jnp.broadcast_to((when < length).astype(f32)[:, None], (ROWS, 128))
    prm = jnp.concatenate([depth_kernel[:, 0], norm_gain, out_gain, jnp.zeros((2, 7, D), f32)], axis=1)
    got = run(x, mask, prm, lift_weight[:, 0])
    t = jnp.arange(frames, dtype=jnp.int32)
    cut = frames // 2
    source = jnp.where(t < cut, local_row(t), ROWS + local_row(t - late))
    back = (source[:, None] == jnp.arange(2 * ROWS, dtype=jnp.int32)[None]).astype(jnp.bfloat16)
    got = got.reshape(2, 2 * ROWS, D // 4)
    return jnp.stack([jnp.dot(back, got[c], preferred_element_type=f32).astype(jnp.bfloat16) for c in range(2)])

def local_row(t):
    return t % SEG * LANES + t // SEG

def solution(mesh):
    return jax.shard_map(
        on_device,
        mesh=mesh,
        in_specs=(P("dp", None, None), P("dp"), P(None, "pipe", None), P(None, "pipe", "dp", None), P(None, "pipe", None, None), P(None, "pipe", None)),
        out_specs=P("dp", None, "pipe"),
        check_vma=False,
    )
```

```python
import functools

import jax
import jax.numpy as jnp
from jax import lax
from jax.experimental import pallas as pl
from jax.experimental.pallas import tpu as pltpu
from jax.sharding import PartitionSpec as P

ROWS = 384; LANES = 16; SEG = ROWS // LANES; D = 1536; TAPS = 31; HALF = 15; EPS = 1e-5
f32 = jnp.float32
bf16 = jnp.bfloat16
GROUP, NB = 8, 8

def sigm(v):
    return 1.0 / (1.0 + jnp.exp(-v))

class Module:
    def __init__(s, st, mask, prm, wb, norm, gpads, mix):
        s.st, s.mask, s.prm, s.wb, s.norm, s.gpads, s.mix = st, mask, prm, wb, norm, gpads, mix
    def edges(s, g, box, send, recv):
        s.g, s.box, s.esend, s.erecv = g, box, send, recv
    def edge(s, m, j, core):
        over = s.over
        part = s.gpads[j % 3].at[:, 16 + over:31 + over, 0:8] if core == 1 else s.gpads[j % 3].at[:, 16 + SEG - over - HALF:16 + SEG - over, 8:16]
        slot = lax.rem(m, jnp.int32(2))
        return pltpu.make_async_remote_copy(part, s.box.at[slot, j], s.esend.at[slot, j], s.erecv.at[slot, j], device_id=dev(s.g.x, s.g.y, s.g.z, 1 - s.g.core), device_id_type=MESH)
    def give(s, m, j):
        for core in range(2):
            @pl.when(s.g.core == core)
            def _(): s.edge(m, j, core).start()
    def take(s, m, j):
        slot = lax.rem(m, jnp.int32(2)); pad = s.gpads[j % 3]
        for core in range(2):
            @pl.when(s.g.core == core)
            def _():
                s.edge(m, j, core).wait()
                if core == 0: pad[:, 16 + SEG:31 + SEG, LANES - 1:LANES] = s.box[slot, j, :, :, 0:1]
                else: pad[:, 1:16, 0:1] = s.box[slot, j, :, :, 7:8]
    def taps(s, m):
        return s.prm[0].at[lax.rem(m, jnp.int32(4)), lax.div(m, jnp.int32(4))]
    def gain(s, m, row):
        return s.prm[1][lax.rem(m, jnp.int32(4)), lax.div(m, jnp.int32(4)), row:row + 1, :]
    def ln1(s, m):
        gain = s.gain(m, 0)
        @pl.loop(0, ROWS // 32)
        def _(r):
            for h in range(2):
                rows = pl.ds(pl.multiple_of(r * 32 + h * 16, 16), 16)
                v = s.st[rows, :].astype(f32)
                v = v - jnp.mean(v, axis=-1, keepdims=True)
                q = lax.rsqrt(jnp.mean(v * v, axis=-1, keepdims=True) + EPS) * s.mask[rows, :1]
                s.norm[rows, :] = (v * q * gain).astype(bf16)
    def lift(s, m, j):
        slot = lax.rem(m, jnp.int32(2)); pad = s.gpads[j % 3]
        w = lambda c: s.wb[slot, :, :, :, :, c:c + 256].reshape(D, 256)
        a = jnp.dot(s.norm[...], w(j * 256), preferred_element_type=f32)
        b = jnp.dot(s.norm[...], w(D + j * 256), preferred_element_type=f32)
        sub = lax.broadcasted_iota(jnp.int32, (HALF, LANES, 128), 1)
        for q in range(2):
            l = slice(q * 128, q * 128 + 128)
            g = (a[:, l] * sigm(b[:, l])).reshape(SEG, LANES, 128)
            pad[q, 16:16 + SEG] = g
            pad[q, 1:16] = jnp.where(sub == 0, 0.0, pltpu.roll(g[SEG - HALF:], 1, 1))
            pad[q, 16 + SEG:31 + SEG] = jnp.where(sub == LANES - 1, 0.0, pltpu.roll(g[:HALF], LANES - 1, 1))
    def conv(s, m, j):
        pad = s.gpads[j % 3]
        for q in range(2):
            c = slice(j * 256 + q * 128, j * 256 + q * 128 + 128)
            taps = s.taps(m)
            w = [jnp.broadcast_to(taps[k:k + 1, c], (LANES, 128)).astype(bf16) for k in range(TAPS)]
            for base in range(0, SEG, NB):
                acc = [None] * NB
                x = {}
                for k0 in range(0, TAPS, GROUP):
                    ks = range(k0, min(TAPS, k0 + GROUP))
                    for t in range(k0, k0 + len(ks) + NB - 1):
                        if t not in x: x[t] = pad[q, base + 1 + t].astype(bf16)
                    for o in range(NB):
                        p = None
                        for k in ks:
                            p = x[o + k] * w[k] if p is None else p + x[o + k] * w[k]
                        p = p.astype(f32)
                        acc[o] = p if acc[o] is None else acc[o] + p
                for o in range(NB):
                    s.mix[base + o, :, c] = acc[o]
    def ln2(s, m):
        gain = s.gain(m, 1)
        @pl.loop(0, ROWS // 32)
        def _(r):
            for h in range(2):
                rows = pl.ds(pl.multiple_of(r * 32 + h * 16, 16), 16)
                v = s.mix[r * 2 + h]
                v = v - jnp.mean(v, axis=-1, keepdims=True)
                q = lax.rsqrt(jnp.mean(v * v, axis=-1, keepdims=True) + EPS)
                y = v * q * gain
                s.st[rows, :] = (s.st[rows, :].astype(f32) + s.mask[rows, :1] * (y * sigm(y))).astype(bf16)
    def stage(s, m, j):
        if j >= 2:
            s.take(m, j - 2)
            s.conv(m, j - 2)
        if j < 6:
            s.lift(m, j)
            s.give(m, j)
    def run(s, m):
        s.ln1(m)
        for j in range(8): s.stage(m, j)
        s.ln2(m)


SPLIT = (4, 5, 3)
MESH = pl.DeviceIdType.MESH

def div(a, b): return lax.div(a, jnp.int32(b))

def rem(a, b): return lax.rem(a, jnp.int32(b))

def coords():
    pipe = lax.axis_index("pipe"); dp = lax.axis_index("dp")
    return rem(div(dp, 4), 4), rem(dp, 4), div(pipe, 2) * 2 + div(dp, 16), rem(pipe, 2)

def dev(x, y, z, core):
    return {"pipe": div(z, 2) * 2 + core, "dp": rem(z, 2) * 16 + x * 4 + y}

class Ring:
    def __init__(s, pos, at, unit, half, present, send, recv):
        s.pos, s.at, s.unit, s.half, s.present, s.send, s.recv = pos, at, unit, half, present, send, recv
    def copy(s, k, src, to):
        return pltpu.make_async_remote_copy(src, src, s.send.at[k], s.recv.at[k], device_id=s.at(to), device_id_type=MESH)
    def sends(s):
        p = s.pos; up, dn = rem(p + 1, 4), rem(p + 3, 4)
        return [(s.present(p), lambda: s.copy(0, s.unit(p), up)), (s.present(p), lambda: s.copy(1, s.unit(p), dn)),
                (s.present(dn), lambda: s.copy(2, s.half(dn, 0), up)), (s.present(up), lambda: s.copy(3, s.half(up, 1), dn))]
    def recvs(s):
        p = s.pos; up, dn, op = rem(p + 1, 4), rem(p + 3, 4), rem(p + 2, 4)
        return [(s.present(dn), lambda: s.copy(0, s.unit(dn), up)), (s.present(up), lambda: s.copy(1, s.unit(up), dn)),
                (s.present(op), lambda: s.copy(2, s.half(op, 0), up)), (s.present(op), lambda: s.copy(3, s.half(op, 1), dn))]

def do(item, what):
    cond, mk = item
    if cond is True:
        getattr(mk(), what)()
    else:
        @pl.when(cond)
        def _(): getattr(mk(), what)()

class Gather:
    def __init__(s, w_ref, full, sems):
        s.w, s.full = w_ref, full
        s.x, s.y, s.z, s.core = coords()
        s.zl, s.zh = rem(s.z, 2), div(s.z, 2)
        s.sec = s.zh * 2 + s.core
        (s.own_sem, s.zs, s.zr, s.cs, s.cr, s.ms, s.mr, s.fs, s.fr, s.ds, s.dr) = sems
    def cols(s, part, n=1, core=None):
        core = s.core if core is None else core
        return pl.ds(pl.multiple_of(core * 1536 + 128 * sum(SPLIT[:part]), 128), 128 * sum(SPLIT[part:part + n]))
    def peers(s):
        x, y, z, c = s.x, s.y, s.z, s.core
        r = [dev(x, y, z, 1 - c)]
        r += [dev(rem(x + d, 4), y, z, c) for d in (1, 2, 3)]
        r += [dev(x, rem(y + d, 4), z, c) for d in (1, 3)]
        r += [dev(x, y, rem(z + d, 4), c) for d in (1, 2, 3)]
        r += [dev(x, y, rem(z + 2, 4), 1 - c)]
        return r
    def own_copies(s):
        o = 1 - s.core
        mine, other = s.cols(0, 3), s.cols(0, 3, o)
        here = s.full.at[:, s.sec, s.zl, s.x, s.y]
        return (pltpu.make_async_copy(s.w.at[:, :, mine], here.at[:, :, mine], s.own_sem.at[0]),
                pltpu.make_async_remote_copy(s.w.at[:, :, other], here.at[:, :, other], s.own_sem.at[1], s.own_sem.at[2], device_id=dev(s.x, s.y, s.z, o), device_id_type=MESH))
    def own_arrival(s):
        mine = s.cols(0, 3)
        there = s.full.at[:, s.zh * 2 + 1 - s.core, s.zl, s.x, s.y]
        return pltpu.make_async_remote_copy(s.w.at[:, :, mine], there.at[:, :, mine], s.own_sem.at[1], s.own_sem.at[2], device_id=dev(s.x, s.y, s.z, 1 - s.core), device_id_type=MESH)
    def begin(s):
        a, b = s.own_copies()
        a.start(); b.start(); a.wait(); b.wait_send(); s.own_arrival().wait_recv()
    def mod(s, c):
        return s.full.at[div(c, 4), rem(c, 4)]
    def src(s, c):
        return s.zh == div(rem(c, 4), 2)
    def first_sends(s, c):
        W = s.mod(c); out = []
        for d in (1, 2, 3):
            out.append((s.src(c), functools.partial(s.zcopy, W, c, s.zl, d - 1, rem(s.z + d, 4))))
        for d in (1, 2, 3):
            out.append((s.src(c), functools.partial(s.ccopy, W, c, s.x, d - 1, rem(s.x + d, 4))))
        return out
    def zcopy(s, W, c, zl, k, to):
        sl = W.at[zl, s.x, s.y, :, s.cols(0, 2)]
        return pltpu.make_async_remote_copy(sl, sl, s.zs.at[c, k], s.zr.at[c, zl], device_id=dev(s.x, s.y, to, s.core), device_id_type=MESH)
    def ccopy(s, W, c, q, k, to):
        sl = W.at[s.zl, q, s.y, :, s.cols(2)]
        return pltpu.make_async_remote_copy(sl, sl, s.cs.at[c, k], s.cr.at[c, k], device_id=dev(to, s.y, s.z, s.core), device_id_type=MESH)
    def first_recvs(s, c):
        W = s.mod(c); out = []
        for zl in (0, 1):
            out.append((jnp.logical_not(jnp.logical_and(s.src(c), s.zl == zl)), functools.partial(s.zcopy, W, c, zl, 0, s.z)))
        for d in (1, 2, 3):
            out.append((s.src(c), functools.partial(s.ccopy, W, c, rem(s.x + 4 - d, 4), d - 1, s.x)))
        return out
    def mids(s, c):
        W = s.mod(c); yes = lambda q: True; src = lambda q: s.src(c)
        a, b, cc = s.cols(0), s.cols(1), s.cols(2)
        atx = lambda q: dev(q, s.y, s.z, s.core)
        aty = lambda q: dev(s.x, q, s.z, s.core)
        return [Ring(s.x, atx, lambda q: W.at[:, q, s.y, :, a], lambda q, h: W.at[h, q, s.y, :, a], yes, s.ms.at[c, 0], s.mr.at[c, 0]),
                Ring(s.y, aty, lambda q: W.at[:, s.x, q, :, b], lambda q, h: W.at[h, s.x, q, :, b], yes, s.ms.at[c, 1], s.mr.at[c, 1]),
                Ring(s.y, aty, lambda q: W.at[s.zl, :, q, :, cc], lambda q, h: W.at[s.zl, pl.ds(2 * h, 2), q, :, cc], src, s.ms.at[c, 2], s.mr.at[c, 2])]
    def fins(s, c):
        W = s.mod(c); yes = lambda q: True
        a, b, cc = s.cols(0), s.cols(1), s.cols(2)
        atx = lambda q: dev(q, s.y, s.z, s.core)
        aty = lambda q: dev(s.x, q, s.z, s.core)
        atz = lambda q: dev(s.x, s.y, q, s.core)
        return [Ring(s.y, aty, lambda q: W.at[:, :, q, :, a], lambda q, h: W.at[h, :, q, :, a], yes, s.fs.at[c, 0], s.fr.at[c, 0]),
                Ring(s.x, atx, lambda q: W.at[:, q, :, :, b], lambda q, h: W.at[h, q, :, :, b], yes, s.fs.at[c, 1], s.fr.at[c, 1]),
                Ring(s.z, atz, lambda q: W.at[rem(q, 2), :, :, :, cc], lambda q, h: W.at[rem(q, 2), pl.ds(2 * h, 2), :, :, cc],
                     lambda q: div(q, 2) == div(rem(c, 4), 2), s.fs.at[c, 2], s.fr.at[c, 2])]
    def swap(s, c, part, core):
        sl = s.mod(c).at[:, :, :, :, s.cols(part, 1, core)]
        return pltpu.make_async_remote_copy(sl, sl, s.ds.at[c, part], s.dr.at[c, part], device_id=dev(s.x, s.y, s.z, 1 - s.core), device_id_type=MESH)
    def e1(s, c):
        for it in s.first_sends(c): do(it, "start")
    def e2(s, c):
        for it in s.first_recvs(c): do(it, "wait_recv")
        for r in s.mids(c):
            for it in r.sends()[:2]: do(it, "start")
    def relay(s, rings):
        for k in (0, 1):
            for r in rings:
                do(r.recvs()[k], "wait_recv"); do(r.sends()[2 + k], "start")
    def e3(s, c): s.relay(s.mids(c))
    def e4(s, c):
        for r, f in zip(s.mids(c), s.fins(c)):
            for it in r.recvs()[2:]: do(it, "wait_recv")
            for it in f.sends()[:2]: do(it, "start")
    def e5a(s, c): s.relay(s.fins(c))
    def e5b(s, c):
        for p, r in enumerate(s.fins(c)):
            for it in r.recvs()[2:]: do(it, "wait_recv")
            s.swap(c, p, s.core).start()
    def e6(s, c):
        for p in range(3): s.swap(c, p, 1 - s.core).wait_recv()
    def drain(s, c):
        for it in s.first_sends(c): do(it, "wait_send")
        for r in s.mids(c) + s.fins(c):
            for it in r.sends(): do(it, "wait_send")
        for p in range(3): s.swap(c, p, s.core).wait_send()


def guard(m, fn):
    @pl.when(jnp.logical_and(m >= 0, m < 8))
    def _(): fn(m)

class Tables:
    def __init__(s, g, mine, full, send, recv):
        s.g, s.mine, s.full, s.send, s.recv = g, mine, full, send, recv
        s.far = dev(g.x, g.y, rem(g.z + 2, 4), g.core)
        s.near = dev(g.x, g.y, g.z, 1 - g.core)
        s.across = (1 - g.zh) * 2 + g.core
    def copy(s, k, n, src, section, to):
        return pltpu.make_async_remote_copy(src, s.full[n].at[section], s.send.at[k, n], s.recv.at[k, n], device_id=to, device_id_type=MESH)
    def start(s):
        for n in range(2):
            s.copy(0, n, s.mine[n], s.g.sec, s.far).start(); s.copy(1, n, s.mine[n], s.g.sec, s.near).start()
            s.full[n][s.g.sec] = s.mine[n][...]
    def relay(s):
        for n in range(2):
            s.copy(0, n, s.mine[n], s.across, s.far).wait_recv()
            s.copy(2, n, s.full[n].at[s.across], s.across, s.near).start()
    def finish(s):
        o = 1 - s.g.core
        for n in range(2):
            s.copy(1, n, s.mine[n], s.g.zh * 2 + o, s.near).wait_recv()
            s.copy(2, n, s.mine[n], (1 - s.g.zh) * 2 + o, s.near).wait_recv()
            for k in range(3): s.copy(k, n, s.mine[n], s.g.sec, s.near).wait_send()

class Shares:
    def __init__(s, g, send, recv, own):
        s.g, s.send, s.recv, s.own = g, send, recv, own
    def each(s, src_of, dst_of, what):
        me = s.g.sec
        for q in range(4):
            if what == "start":
                @pl.when(me != q)
                def _(): pltpu.make_async_remote_copy(src_of(q), dst_of(me), s.send.at[q], s.recv.at[me], device_id={"pipe": q}, device_id_type=MESH).start()
                @pl.when(me == q)
                def _(): pltpu.make_async_copy(src_of(q), dst_of(me), s.own).start()
            else:
                @pl.when(me != q)
                def _():
                    pltpu.make_async_remote_copy(src_of(q), dst_of(me), s.send.at[q], s.recv.at[me], device_id={"pipe": q}, device_id_type=MESH).wait_send()
                    pltpu.make_async_remote_copy(src_of(q), dst_of(q), s.send.at[q], s.recv.at[q], device_id={"pipe": q}, device_id_type=MESH).wait_recv()
                @pl.when(me == q)
                def _(): pltpu.make_async_copy(src_of(q), dst_of(me), s.own).wait()

def kernel(x_ref, mask_ref, taps_ref, gain_ref, w_ref, out_ref, full, st, wb, norm, gpa, gpb, gpc, mix, wsem, taps_all, gain_all, taps_wide, ps, pr, os_, or_, oo, xin, xsem, box, es, er, *sems):
    g = Gather(w_ref, full, sems)
    b = pltpu.get_barrier_semaphore()
    for d in g.peers():
        pl.semaphore_signal(b, inc=1, device_id=d, device_id_type=MESH)
    pl.semaphore_wait(b, len(g.peers()))
    tables = Tables(g, (taps_ref, gain_ref), (taps_all, gain_all), ps, pr)
    g.begin()
    g.e1(jnp.int32(0))
    tables.start()
    clip = pltpu.make_async_copy(x_ref.at[g.zh], xin, xsem)
    clip.start()
    clip.wait()
    frames = xin.shape[0]
    p = lax.broadcasted_iota(jnp.int32, (ROWS, frames), 0)
    when = rem(p, LANES) * SEG + div(p, LANES) + g.core * (frames - ROWS)
    norm_pick = (when == lax.broadcasted_iota(jnp.int32, (ROWS, frames), 1)).astype(bf16)
    for j in range(6):
        c = slice(256 * j, 256 * j + 256)
        st[:, c] = jnp.dot(norm_pick, xin[:, c], preferred_element_type=f32).astype(bf16)
    md = Module(st, mask_ref, (taps_wide, gain_all), wb, norm, (gpa, gpb, gpc), mix)
    md.over = 2 * ROWS - x_ref.shape[1]
    md.edges(g, box, es, er)
    load = lambda m: pltpu.make_async_copy(full.at[div(m, 4), rem(m, 4)], wb.at[rem(m, 2)], wsem.at[rem(m, 2)])
    def ready():
        tables.finish()
        taps_wide[...] = taps_all[...].astype(f32)
    def some(m, lo, hi):
        for j in range(lo, hi): md.stage(m, j)
    @pl.loop(0, 14)
    def _(i):
        m = i - 6
        @pl.when(i == 2)
        def _(): tables.relay()
        @pl.when(i == 5)
        def _(): ready()
        guard(m, lambda m: (g.e6(m), load(m).start()))
        @pl.when(i > 0)
        def _(): guard(i, g.e1)
        guard(i - 1, g.e2); guard(i - 2, g.e3); guard(i - 3, g.e4); guard(i - 4, g.e5a); guard(i - 5, g.e5b)
        @pl.when(m >= 0)
        def _():
            md.ln1(m); load(m).wait(); some(m, 0, 8); md.ln2(m)
    outs = Shares(g, os_, or_, oo)
    osrc, odst = (lambda q: st.at[:, pl.ds(q * (D // 4), D // 4)]), (lambda q: out_ref.at[q])
    outs.each(osrc, odst, "start")
    @pl.loop(0, 8)
    def _(i): g.drain(i)
    outs.each(osrc, odst, "wait")

SEM = pltpu.SemaphoreType.DMA
V = pltpu.VMEM

def run(x, mask, taps, gains, w):
    vm, hbm = pl.BlockSpec(memory_space=pltpu.VMEM), pl.BlockSpec(memory_space=pl.ANY)
    return pl.pallas_call(
        kernel,
        out_shape=(jax.ShapeDtypeStruct((4, ROWS, D // 4), jnp.bfloat16), jax.ShapeDtypeStruct((2, 4, 2, 4, 4, 48, 2 * D), jnp.bfloat16)),
        in_specs=[hbm, vm, vm, vm, vm],
        out_specs=(hbm, hbm),
        scratch_shapes=[
            V((ROWS, D), jnp.bfloat16), V((2, 2, 4, 4, 48, 2 * D), jnp.bfloat16), V((ROWS, D), jnp.bfloat16),
            V((2, 32 + SEG, LANES, 128), f32), V((2, 32 + SEG, LANES, 128), f32), V((2, 32 + SEG, LANES, 128), f32), V((SEG, LANES, D), f32), SEM((2,)), V((4, 2, 32, D), bf16), V((4, 2, 8, D), f32), V((4, 2, 32, D), f32),
            SEM((3, 2)), SEM((3, 2)), SEM((4,)), SEM((4,)), SEM, V(x.shape[1:], bf16), SEM, V((2, 6, 2, HALF, 8, 128), f32), SEM((2, 6)), SEM((2, 6)),
            SEM((3,)), SEM((8, 3)), SEM((8, 2)), SEM((8, 3)), SEM((8, 3)), SEM((8, 3, 4)), SEM((8, 3, 4)), SEM((8, 3, 4)), SEM((8, 3, 4)), SEM((8, 3)), SEM((8, 3)),
        ],
        compiler_params=pltpu.CompilerParams(collective_id=0, has_side_effects=True, vmem_limit_bytes=60 * 2**20),
    )(x, mask, taps, gains, w)[0]

def on_device(frames_in, lengths, norm_gain, lift_weight, depth_kernel, out_gain):
    frames = frames_in.shape[1]
    pipe = lax.axis_index("pipe")
    clip, half = pipe // 2, pipe % 2
    late = frames - ROWS
    p = jnp.arange(ROWS, dtype=jnp.int32)
    local = p % LANES * SEG + p // LANES
    when = local + half * late
    length = lax.dynamic_index_in_dim(lengths, clip, 0, keepdims=False)
    mask = jnp.broadcast_to((when < length).astype(f32)[:, None], (ROWS, 128))
    taps = jnp.pad(depth_kernel[:, 0].astype(bf16), ((0, 0), (0, 1), (0, 0)))
    gains = jnp.concatenate([norm_gain, out_gain, jnp.zeros((2, 6, D), f32)], axis=1)
    got = run(frames_in, mask, taps, gains, lift_weight[:, 0])
    t = jnp.arange(frames, dtype=jnp.int32)
    cut = frames // 2
    source = jnp.where(t < cut, local_row(t), ROWS + local_row(t - late))
    back = (source[:, None] == jnp.arange(2 * ROWS, dtype=jnp.int32)[None]).astype(jnp.bfloat16)
    got = got.reshape(2, 2 * ROWS, D // 4)
    return jnp.stack([jnp.dot(back, got[c], preferred_element_type=f32).astype(jnp.bfloat16) for c in range(2)])

def local_row(t):
    return t % SEG * LANES + t // SEG

def solution(mesh):
    return jax.shard_map(
        on_device,
        mesh=mesh,
        in_specs=(P("dp", None, None), P("dp"), P(None, "pipe", None), P(None, "pipe", "dp", None), P(None, "pipe", None, None), P(None, "pipe", None)),
        out_specs=P("dp", None, "pipe"),
        check_vma=False,
    )
```

```python
import functools

import jax
import jax.numpy as jnp
from jax import lax
from jax.experimental import pallas as pl
from jax.experimental.pallas import tpu as pltpu
from jax.sharding import PartitionSpec as P

ROWS = 384; LANES = 16; SEG = ROWS // LANES; D = 1536; TAPS = 31; HALF = 15; EPS = 1e-5
f32 = jnp.float32
bf16 = jnp.bfloat16
GROUP, NB = 8, 8

def sigm(v):
    return 1.0 / (1.0 + jnp.exp(-v))

class Module:
    def __init__(s, st, mask, prm, wb, norm, gpads, mix):
        s.st, s.mask, s.prm, s.wb, s.norm, s.gpads, s.mix = st, mask, prm, wb, norm, gpads, mix
    def edges(s, g, box, send, recv):
        s.g, s.box, s.esend, s.erecv = g, box, send, recv
    def edge(s, m, j, core):
        over = s.over
        part = s.gpads[j % 3].at[:, 16 + over:31 + over, 0:8] if core == 1 else s.gpads[j % 3].at[:, 16 + SEG - over - HALF:16 + SEG - over, 8:16]
        slot = lax.rem(m, jnp.int32(2))
        return pltpu.make_async_remote_copy(part, s.box.at[slot, j], s.esend.at[slot, j], s.erecv.at[slot, j], device_id=dev(s.g.x, s.g.y, s.g.z, 1 - s.g.core), device_id_type=MESH)
    def give(s, m, j):
        for core in range(2):
            @pl.when(s.g.core == core)
            def _(): s.edge(m, j, core).start()
    def take(s, m, j):
        slot = lax.rem(m, jnp.int32(2)); pad = s.gpads[j % 3]
        for core in range(2):
            @pl.when(s.g.core == core)
            def _():
                s.edge(m, j, core).wait()
                if core == 0: pad[:, 16 + SEG:31 + SEG, LANES - 1:LANES] = s.box[slot, j, :, :, 0:1]
                else: pad[:, 1:16, 0:1] = s.box[slot, j, :, :, 7:8]
    def taps(s, m):
        return s.prm[0].at[lax.rem(m, jnp.int32(4)), lax.div(m, jnp.int32(4))]
    def gain(s, m, row):
        return s.prm[1][lax.rem(m, jnp.int32(4)), lax.div(m, jnp.int32(4)), row:row + 1, :]
    def ln1(s, m):
        gain = s.gain(m, 0)
        @pl.loop(0, ROWS // 32)
        def _(r):
            for h in range(2):
                rows = pl.ds(pl.multiple_of(r * 32 + h * 16, 16), 16)
                v = s.st[rows, :].astype(f32)
                v = v - jnp.mean(v, axis=-1, keepdims=True)
                q = lax.rsqrt(jnp.mean(v * v, axis=-1, keepdims=True) + EPS) * s.mask[rows, :1]
                s.norm[rows, :] = (v * q * gain).astype(bf16)
    def lift(s, m, j):
        slot = lax.rem(m, jnp.int32(2)); pad = s.gpads[j % 3]
        w = lambda c: s.wb[slot, :, :, :, :, c:c + 256].reshape(D, 256)
        a = jnp.dot(s.norm[...], w(j * 256), preferred_element_type=f32)
        b = jnp.dot(s.norm[...], w(D + j * 256), preferred_element_type=f32)
        sub = lax.broadcasted_iota(jnp.int32, (HALF, LANES, 128), 1)
        for q in range(2):
            l = slice(q * 128, q * 128 + 128)
            g = (a[:, l] * sigm(b[:, l])).reshape(SEG, LANES, 128)
            pad[q, 16:16 + SEG] = g
            pad[q, 1:16] = jnp.where(sub == 0, 0.0, pltpu.roll(g[SEG - HALF:], 1, 1))
            pad[q, 16 + SEG:31 + SEG] = jnp.where(sub == LANES - 1, 0.0, pltpu.roll(g[:HALF], LANES - 1, 1))
    def conv(s, m, j):
        pad = s.gpads[j % 3]
        for q in range(2):
            c = slice(j * 256 + q * 128, j * 256 + q * 128 + 128)
            taps = s.taps(m)
            w = [jnp.broadcast_to(taps[k:k + 1, c], (LANES, 128)).astype(bf16) for k in range(TAPS)]
            for base in range(0, SEG, NB):
                acc = [None] * NB
                x = {}
                for k0 in range(0, TAPS, GROUP):
                    ks = range(k0, min(TAPS, k0 + GROUP))
                    for t in range(k0, k0 + len(ks) + NB - 1):
                        if t not in x: x[t] = pad[q, base + 1 + t].astype(bf16)
                    for o in range(NB):
                        p = None
                        for k in ks:
                            p = x[o + k] * w[k] if p is None else p + x[o + k] * w[k]
                        p = p.astype(f32)
                        acc[o] = p if acc[o] is None else acc[o] + p
                for o in range(NB):
                    s.mix[base + o, :, c] = acc[o]
    def ln2(s, m):
        gain = s.gain(m, 1)
        @pl.loop(0, ROWS // 32)
        def _(r):
            for h in range(2):
                rows = pl.ds(pl.multiple_of(r * 32 + h * 16, 16), 16)
                v = s.mix[r * 2 + h]
                v = v - jnp.mean(v, axis=-1, keepdims=True)
                q = lax.rsqrt(jnp.mean(v * v, axis=-1, keepdims=True) + EPS)
                y = v * q * gain
                s.st[rows, :] = (s.st[rows, :].astype(f32) + s.mask[rows, :1] * (y * sigm(y))).astype(bf16)
    def stage(s, m, j):
        if j >= 2:
            s.take(m, j - 2)
            s.conv(m, j - 2)
        if j < 6:
            s.lift(m, j)
            s.give(m, j)
    def run(s, m):
        s.ln1(m)
        for j in range(8): s.stage(m, j)
        s.ln2(m)


SPLIT = ((2, 3, 1), (2, 2, 2))
MESH = pl.DeviceIdType.MESH

def div(a, b): return lax.div(a, jnp.int32(b))

def rem(a, b): return lax.rem(a, jnp.int32(b))

def coords():
    pipe = lax.axis_index("pipe"); dp = lax.axis_index("dp")
    return rem(div(dp, 4), 4), rem(dp, 4), div(pipe, 2) * 2 + div(dp, 16), rem(pipe, 2)

def dev(x, y, z, core):
    return {"pipe": div(z, 2) * 2 + core, "dp": rem(z, 2) * 16 + x * 4 + y}

class Ring:
    def __init__(s, pos, at, unit, half, present, send, recv):
        s.pos, s.at, s.unit, s.half, s.present, s.send, s.recv = pos, at, unit, half, present, send, recv
    def copy(s, k, src, to):
        return pltpu.make_async_remote_copy(src, src, s.send.at[k], s.recv.at[k], device_id=s.at(to), device_id_type=MESH)
    def sends(s):
        p = s.pos; up, dn = rem(p + 1, 4), rem(p + 3, 4)
        return [(s.present(p), lambda: s.copy(0, s.unit(p), up)), (s.present(p), lambda: s.copy(1, s.unit(p), dn)),
                (s.present(dn), lambda: s.copy(2, s.half(dn, 0), up)), (s.present(up), lambda: s.copy(3, s.half(up, 1), dn))]
    def recvs(s):
        p = s.pos; up, dn, op = rem(p + 1, 4), rem(p + 3, 4), rem(p + 2, 4)
        return [(s.present(dn), lambda: s.copy(0, s.unit(dn), up)), (s.present(up), lambda: s.copy(1, s.unit(up), dn)),
                (s.present(op), lambda: s.copy(2, s.half(op, 0), up)), (s.present(op), lambda: s.copy(3, s.half(op, 1), dn))]

def do(item, what):
    cond, mk = item
    if cond is True:
        getattr(mk(), what)()
    else:
        @pl.when(cond)
        def _(): getattr(mk(), what)()

class Gather:
    def __init__(s, w_ref, full, sems):
        s.w, s.full = w_ref, full
        s.x, s.y, s.z, s.core = coords()
        s.zl, s.zh = rem(s.z, 2), div(s.z, 2)
        s.sec = s.zh * 2 + s.core
        (s.own_sem, s.zs, s.zr, s.cs, s.cr, s.ms, s.mr, s.fs, s.fr, s.ds, s.dr) = sems
    def cols(s, part, n=1, core=None):
        core = s.core if core is None else core
        split = SPLIT[s.half]
        return pl.ds(pl.multiple_of(core * D + s.half * (D // 2) + 128 * sum(split[:part]), 128), 128 * sum(split[part:part + n]))
    def side(s, core):
        return pl.ds(pl.multiple_of(core * D, 128), D)
    def peers(s):
        x, y, z, c = s.x, s.y, s.z, s.core
        r = [dev(x, y, z, 1 - c)]
        r += [dev(rem(x + d, 4), y, z, c) for d in (1, 2, 3)]
        r += [dev(x, rem(y + d, 4), z, c) for d in (1, 3)]
        r += [dev(x, y, rem(z + d, 4), c) for d in (1, 2, 3)]
        r += [dev(x, y, rem(z + 2, 4), 1 - c)]
        return r
    def own_copies(s):
        o = 1 - s.core
        mine, other = s.side(s.core), s.side(o)
        here = s.full.at[:, s.sec, s.zl, s.x, s.y]
        return (pltpu.make_async_copy(s.w.at[:, :, mine], here.at[:, :, mine], s.own_sem.at[0]),
                pltpu.make_async_remote_copy(s.w.at[:, :, other], here.at[:, :, other], s.own_sem.at[1], s.own_sem.at[2], device_id=dev(s.x, s.y, s.z, o), device_id_type=MESH))
    def own_arrival(s):
        mine = s.side(s.core)
        there = s.full.at[:, s.zh * 2 + 1 - s.core, s.zl, s.x, s.y]
        return pltpu.make_async_remote_copy(s.w.at[:, :, mine], there.at[:, :, mine], s.own_sem.at[1], s.own_sem.at[2], device_id=dev(s.x, s.y, s.z, 1 - s.core), device_id_type=MESH)
    def begin(s):
        a, b = s.own_copies()
        a.start(); b.start(); a.wait(); b.wait_send(); s.own_arrival().wait_recv()
    def mod(s, c):
        return s.full.at[div(c, 8), rem(div(c, 2), 4)]
    def src(s, c):
        return s.zh == div(rem(div(c, 2), 4), 2)
    def first_sends(s, c):
        W = s.mod(c); out = []
        for d in (1, 2, 3):
            out.append((s.src(c), functools.partial(s.zcopy, W, c, s.zl, d - 1, rem(s.z + d, 4))))
        for d in (1, 2, 3):
            out.append((s.src(c), functools.partial(s.ccopy, W, c, s.x, d - 1, rem(s.x + d, 4))))
        return out
    def zcopy(s, W, c, zl, k, to):
        sl = W.at[zl, s.x, s.y, :, s.cols(0, 2)]
        return pltpu.make_async_remote_copy(sl, sl, s.zs.at[c, k], s.zr.at[c, zl], device_id=dev(s.x, s.y, to, s.core), device_id_type=MESH)
    def ccopy(s, W, c, q, k, to):
        sl = W.at[s.zl, q, s.y, :, s.cols(2)]
        return pltpu.make_async_remote_copy(sl, sl, s.cs.at[c, k], s.cr.at[c, k], device_id=dev(to, s.y, s.z, s.core), device_id_type=MESH)
    def first_recvs(s, c):
        W = s.mod(c); out = []
        for zl in (0, 1):
            out.append((jnp.logical_not(jnp.logical_and(s.src(c), s.zl == zl)), functools.partial(s.zcopy, W, c, zl, 0, s.z)))
        for d in (1, 2, 3):
            out.append((s.src(c), functools.partial(s.ccopy, W, c, rem(s.x + 4 - d, 4), d - 1, s.x)))
        return out
    def mids(s, c):
        W = s.mod(c); yes = lambda q: True; src = lambda q: s.src(c)
        a, b, cc = s.cols(0), s.cols(1), s.cols(2)
        atx = lambda q: dev(q, s.y, s.z, s.core)
        aty = lambda q: dev(s.x, q, s.z, s.core)
        return [Ring(s.x, atx, lambda q: W.at[:, q, s.y, :, a], lambda q, h: W.at[h, q, s.y, :, a], yes, s.ms.at[c, 0], s.mr.at[c, 0]),
                Ring(s.y, aty, lambda q: W.at[:, s.x, q, :, b], lambda q, h: W.at[h, s.x, q, :, b], yes, s.ms.at[c, 1], s.mr.at[c, 1]),
                Ring(s.y, aty, lambda q: W.at[s.zl, :, q, :, cc], lambda q, h: W.at[s.zl, pl.ds(2 * h, 2), q, :, cc], src, s.ms.at[c, 2], s.mr.at[c, 2])]
    def fins(s, c):
        W = s.mod(c); yes = lambda q: True
        a, b, cc = s.cols(0), s.cols(1), s.cols(2)
        atx = lambda q: dev(q, s.y, s.z, s.core)
        aty = lambda q: dev(s.x, q, s.z, s.core)
        atz = lambda q: dev(s.x, s.y, q, s.core)
        return [Ring(s.y, aty, lambda q: W.at[:, :, q, :, a], lambda q, h: W.at[h, :, q, :, a], yes, s.fs.at[c, 0], s.fr.at[c, 0]),
                Ring(s.x, atx, lambda q: W.at[:, q, :, :, b], lambda q, h: W.at[h, q, :, :, b], yes, s.fs.at[c, 1], s.fr.at[c, 1]),
                Ring(s.z, atz, lambda q: W.at[rem(q, 2), :, :, :, cc], lambda q, h: W.at[rem(q, 2), pl.ds(2 * h, 2), :, :, cc],
                     lambda q: div(q, 2) == div(rem(div(c, 2), 4), 2), s.fs.at[c, 2], s.fr.at[c, 2])]
    def swap(s, c, part, core):
        sl = s.mod(c).at[:, :, :, :, s.cols(part, 1, core)]
        return pltpu.make_async_remote_copy(sl, sl, s.ds.at[c, part], s.dr.at[c, part], device_id=dev(s.x, s.y, s.z, 1 - s.core), device_id_type=MESH)
    def e1(s, c):
        for it in s.first_sends(c): do(it, "start")
    def e2(s, c):
        for it in s.first_recvs(c): do(it, "wait_recv")
        for r in s.mids(c):
            for it in r.sends()[:2]: do(it, "start")
    def relay(s, rings):
        for k in (0, 1):
            for r in rings:
                do(r.recvs()[k], "wait_recv"); do(r.sends()[2 + k], "start")
    def e3(s, c): s.relay(s.mids(c))
    def e4(s, c):
        for r, f in zip(s.mids(c), s.fins(c)):
            for it in r.recvs()[2:]: do(it, "wait_recv")
            for it in f.sends()[:2]: do(it, "start")
    def e5a(s, c): s.relay(s.fins(c))
    def e5b(s, c):
        for p, r in enumerate(s.fins(c)):
            for it in r.recvs()[2:]: do(it, "wait_recv")
            s.swap(c, p, s.core).start()
    def e6(s, c):
        for p in range(3): s.swap(c, p, 1 - s.core).wait_recv()
    def drain(s, c):
        for it in s.first_sends(c): do(it, "wait_send")
        for r in s.mids(c) + s.fins(c):
            for it in r.sends(): do(it, "wait_send")
        for p in range(3): s.swap(c, p, s.core).wait_send()


def guard(m, fn):
    @pl.when(jnp.logical_and(m >= 0, m < 16))
    def _(): fn(m)

class Tables:
    def __init__(s, g, mine, full, send, recv):
        s.g, s.mine, s.full, s.send, s.recv = g, mine, full, send, recv
        s.far = dev(g.x, g.y, rem(g.z + 2, 4), g.core)
        s.near = dev(g.x, g.y, g.z, 1 - g.core)
        s.across = (1 - g.zh) * 2 + g.core
    def copy(s, k, n, src, section, to):
        return pltpu.make_async_remote_copy(src, s.full[n].at[section], s.send.at[k, n], s.recv.at[k, n], device_id=to, device_id_type=MESH)
    def start(s):
        for n in range(2):
            s.copy(0, n, s.mine[n], s.g.sec, s.far).start(); s.copy(1, n, s.mine[n], s.g.sec, s.near).start()
            s.full[n][s.g.sec] = s.mine[n][...]
    def relay(s):
        for n in range(2):
            s.copy(0, n, s.mine[n], s.across, s.far).wait_recv()
            s.copy(2, n, s.full[n].at[s.across], s.across, s.near).start()
    def finish(s):
        o = 1 - s.g.core
        for n in range(2):
            s.copy(1, n, s.mine[n], s.g.zh * 2 + o, s.near).wait_recv()
            s.copy(2, n, s.mine[n], (1 - s.g.zh) * 2 + o, s.near).wait_recv()
            for k in range(3): s.copy(k, n, s.mine[n], s.g.sec, s.near).wait_send()

class Shares:
    def __init__(s, g, send, recv, own):
        s.g, s.send, s.recv, s.own = g, send, recv, own
    def each(s, src_of, dst_of, what):
        me = s.g.sec
        for q in range(4):
            if what == "start":
                @pl.when(me != q)
                def _(): pltpu.make_async_remote_copy(src_of(q), dst_of(me), s.send.at[q], s.recv.at[me], device_id={"pipe": q}, device_id_type=MESH).start()
                @pl.when(me == q)
                def _(): pltpu.make_async_copy(src_of(q), dst_of(me), s.own).start()
            else:
                @pl.when(me != q)
                def _():
                    pltpu.make_async_remote_copy(src_of(q), dst_of(me), s.send.at[q], s.recv.at[me], device_id={"pipe": q}, device_id_type=MESH).wait_send()
                    pltpu.make_async_remote_copy(src_of(q), dst_of(q), s.send.at[q], s.recv.at[q], device_id={"pipe": q}, device_id_type=MESH).wait_recv()
                @pl.when(me == q)
                def _(): pltpu.make_async_copy(src_of(q), dst_of(me), s.own).wait()

def kernel(x_ref, mask_ref, taps_ref, gain_ref, w_ref, out_ref, full, st, wb, norm, gpa, gpb, gpc, mix, wsem, taps_all, gain_all, taps_wide, ps, pr, os_, or_, oo, xin, xsem, box, es, er, *sems):
    g = Gather(w_ref, full, sems)
    b = pltpu.get_barrier_semaphore()
    for d in g.peers():
        pl.semaphore_signal(b, inc=1, device_id=d, device_id_type=MESH)
    pl.semaphore_wait(b, len(g.peers()))
    tables = Tables(g, (taps_ref, gain_ref), (taps_all, gain_all), ps, pr)
    g.begin()
    g.half = 0
    g.e1(jnp.int32(0))
    tables.start()
    clip = pltpu.make_async_copy(x_ref.at[g.zh], xin, xsem)
    clip.start()
    clip.wait()
    frames = xin.shape[0]
    p = lax.broadcasted_iota(jnp.int32, (ROWS, frames), 0)
    when = rem(p, LANES) * SEG + div(p, LANES) + g.core * (frames - ROWS)
    norm_pick = (when == lax.broadcasted_iota(jnp.int32, (ROWS, frames), 1)).astype(bf16)
    for j in range(6):
        c = slice(256 * j, 256 * j + 256)
        st[:, c] = jnp.dot(norm_pick, xin[:, c], preferred_element_type=f32).astype(bf16)
    md = Module(st, mask_ref, (taps_wide, gain_all), wb, norm, (gpa, gpb, gpc), mix)
    md.over = 2 * ROWS - x_ref.shape[1]
    md.edges(g, box, es, er)
    def load(m, half, what):
        slot = rem(m, 2)
        for k in range(2):
            c = pl.ds(k * D + half * (D // 2), D // 2)
            getattr(pltpu.make_async_copy(full.at[div(m, 4), rem(m, 4), :, :, :, :, c], wb.at[slot, :, :, :, :, c], wsem.at[slot, half, k]), what)()
    def ready():
        tables.finish()
        taps_wide[...] = taps_all[...].astype(f32)
    def some(m, lo, hi):
        for j in range(lo, hi): md.stage(m, j)
    @pl.loop(0, 12)
    def _(i):
        for half in range(2):
            n = 2 * i + half
            part, m = 1 - half, i - 4 + half
            def event(after, fn):
                g.half = (half - after) % 2
                guard(n - after, fn)
            @pl.when(n == 4)
            def _(): tables.relay()
            @pl.when(n == 5)
            def _(): ready()
            def fetch(k):
                g.e6(k)
                load(m, part, "start")
            event(7, fetch)
            @pl.when(n > 0)
            def _(): event(0, g.e1)
            event(1, g.e2)
            event(2, g.e3)
            event(3, g.e4)
            event(4, g.e5a)
            def compute(k):
                if part == 0: md.ln1(m)
                load(m, part, "wait")
                some(m, 3 * part, 3 + 5 * part)
                if part == 1: md.ln2(m)
            event(7, compute)
            event(5, g.e5b)
    outs = Shares(g, os_, or_, oo)
    osrc, odst = (lambda q: st.at[:, pl.ds(q * (D // 4), D // 4)]), (lambda q: out_ref.at[q])
    outs.each(osrc, odst, "start")
    @pl.loop(0, 8)
    def _(i):
        for half in range(2):
            g.half = half
            g.drain(2 * i + half)
    outs.each(osrc, odst, "wait")

SEM = pltpu.SemaphoreType.DMA
V = pltpu.VMEM

def run(x, mask, taps, gains, w):
    vm, hbm = pl.BlockSpec(memory_space=pltpu.VMEM), pl.BlockSpec(memory_space=pl.ANY)
    return pl.pallas_call(
        kernel,
        out_shape=(jax.ShapeDtypeStruct((4, ROWS, D // 4), jnp.bfloat16), jax.ShapeDtypeStruct((2, 4, 2, 4, 4, 48, 2 * D), jnp.bfloat16)),
        in_specs=[hbm, vm, vm, vm, vm],
        out_specs=(hbm, hbm),
        scratch_shapes=[
            V((ROWS, D), jnp.bfloat16), V((2, 2, 4, 4, 48, 2 * D), jnp.bfloat16), V((ROWS, D), jnp.bfloat16),
            V((2, 32 + SEG, LANES, 128), f32), V((2, 32 + SEG, LANES, 128), f32), V((2, 32 + SEG, LANES, 128), f32), V((SEG, LANES, D), f32), SEM((2, 2, 2)), V((4, 2, 32, D), bf16), V((4, 2, 8, D), f32), V((4, 2, 32, D), f32),
            SEM((3, 2)), SEM((3, 2)), SEM((4,)), SEM((4,)), SEM, V(x.shape[1:], bf16), SEM, V((2, 6, 2, HALF, 8, 128), f32), SEM((2, 6)), SEM((2, 6)),
            SEM((3,)), SEM((16, 3)), SEM((16, 2)), SEM((16, 3)), SEM((16, 3)), SEM((16, 3, 4)), SEM((16, 3, 4)), SEM((16, 3, 4)), SEM((16, 3, 4)), SEM((16, 3)), SEM((16, 3)),
        ],
        compiler_params=pltpu.CompilerParams(collective_id=0, has_side_effects=True, vmem_limit_bytes=60 * 2**20),
    )(x, mask, taps, gains, w)[0]

def on_device(frames_in, lengths, norm_gain, lift_weight, depth_kernel, out_gain):
    frames = frames_in.shape[1]
    pipe = lax.axis_index("pipe")
    clip, half = pipe // 2, pipe % 2
    late = frames - ROWS
    p = jnp.arange(ROWS, dtype=jnp.int32)
    local = p % LANES * SEG + p // LANES
    when = local + half * late
    length = lax.dynamic_index_in_dim(lengths, clip, 0, keepdims=False)
    mask = jnp.broadcast_to((when < length).astype(f32)[:, None], (ROWS, 128))
    taps = jnp.pad(depth_kernel[:, 0].astype(bf16), ((0, 0), (0, 1), (0, 0)))
    gains = jnp.concatenate([norm_gain, out_gain, jnp.zeros((2, 6, D), f32)], axis=1)
    got = run(frames_in, mask, taps, gains, lift_weight[:, 0])
    t = jnp.arange(frames, dtype=jnp.int32)
    cut = frames // 2
    source = jnp.where(t < cut, local_row(t), ROWS + local_row(t - late))
    back = (source[:, None] == jnp.arange(2 * ROWS, dtype=jnp.int32)[None]).astype(jnp.bfloat16)
    got = got.reshape(2, 2 * ROWS, D // 4)
    return jnp.stack([jnp.dot(back, got[c], preferred_element_type=f32).astype(jnp.bfloat16) for c in range(2)])

def local_row(t):
    return t % SEG * LANES + t // SEG

def solution(mesh):
    return jax.shard_map(
        on_device,
        mesh=mesh,
        in_specs=(P("dp", None, None), P("dp"), P(None, "pipe", None), P(None, "pipe", "dp", None), P(None, "pipe", None, None), P(None, "pipe", None)),
        out_specs=P("dp", None, "pipe"),
        check_vma=False,
    )
```
